32 devices in a mesh: dp: 4 (over x, core), ref: 8 (over z, y).
Axes of the slice: x: 2, y: 2, z: 4, core: 2. Of those that a mesh axis runs over, the one named last changes fastest.
Arguments:
- candidates: float32 [384, 64], P('ref'), may hold values from -6 to 6
- observed: float32 [8192, 64], P('dp'), may hold values from -6 to 6
- ref_points: float32 [8192, 64], P('ref'), may hold values from -6 to 6
- slab: float32 [8192, 8192], P('dp', 'ref'), may hold values from -0.3125 to 0.3125
- ref_weight: float32 [8192], P('ref'), may hold values from 0.2 to 2
- inv_scale: float32 [64], replicated, may hold values from 0.06 to 0.2
Outputs:
- ascent: float32 [384, 64], P('ref')
- value: float32 [384], P('ref')
The draws below stay inside these ranges and needn't reach their ends.
All inputs are finite; a program needn't handle non-finite values.
Results may differ from the reference program's by a relative error of at most 0.000067.
Values sent between devices are 32-bit elements; how exact they have to be, the bound alone decides.
A program may use at most 64 MiB of HBM per device.

```python
import math
import jax
import jax.numpy as jnp
from jax import lax

FEAT = 64
Q = 384
OBS = 8192
REFS = 8192


def level_of(key, dims, cuts, smallest, high):
    gain, own = 1.0, jax.random.fold_in(key, 6)
    for position, parts in cuts:
        steps = jnp.exp(jax.random.uniform(jax.random.fold_in(own, position), (parts,), jnp.float32, smallest / len(cuts), high / len(cuts)))
        gain = gain * jnp.repeat(steps, dims[position] // parts).reshape([-1 if axis == position else 1 for axis in range(len(dims))])
    return gain


def noise(rng, dims, deviation, reach, cuts=(), dtype=jnp.bfloat16):
    level = level_of(rng, dims, cuts, -0.22, 0.18) if cuts else 1.0
    result = jax.random.normal(rng, dims, jnp.float32) * deviation * level
    return jnp.minimum(jnp.maximum(result, -reach), reach).astype(dtype)


def setup_inputs(seed: int = 0) -> dict:
    key_list = jax.random.split(jax.random.key(seed), 7)
    candidates = noise(key_list[0], (Q, FEAT), 1.0, 6.0, ((0, 8),), jnp.float32)
    observed = noise(key_list[1], (OBS, FEAT), 1.0, 6.0, ((0, 4),), jnp.float32)
    ref_points = noise(key_list[2], (REFS, FEAT), 1.0, 6.0, ((0, 8),), jnp.float32)
    slab = noise(key_list[3], (OBS, REFS), (2.0 / OBS ** 0.5), 0.3125, ((0, 4), (1, 8)), jnp.float32)
    ref_weight = jnp.clip(jnp.exp(math.log(2.0) - 2.3025851 * jax.random.uniform(key_list[4], (REFS,), jnp.float32) ** level_of(key_list[4], (REFS,), ((0, 8),), -0.2, 0.2)), 0.2, 2.0)
    inv_scale = jnp.clip(jnp.exp(jax.random.uniform(key_list[5], (FEAT,), jnp.float32, math.log(0.06), math.log(0.2))), 0.06, 0.2)
    return {"candidates": candidates, "observed": observed, "ref_points": ref_points, "slab": slab, "ref_weight": ref_weight, "inv_scale": inv_scale}


def kernel(first_set, second_set):
    first_norm = lax.optimization_barrier(jnp.sum(first_set * first_set, axis=1))
    second_norm = lax.optimization_barrier(jnp.sum(second_set * second_set, axis=1))
    cross = lax.dot_general(first_set, second_set, (((1,), (1,)), ((), ())), precision=lax.Precision.HIGHEST, preferred_element_type=jnp.float32)
    return jnp.exp(-0.5 * (first_norm[:, None] + second_norm[None, :] - 2.0 * cross))

def reference(candidates, observed, ref_points, slab, ref_weight, inv_scale):
    squared = inv_scale * inv_scale
    k_obs = kernel(candidates * inv_scale, observed * inv_scale)
    k_ref = kernel(candidates * inv_scale, ref_points * inv_scale)
    covar = jnp.dot(k_obs, slab, precision=lax.Precision.HIGHEST, preferred_element_type=jnp.float32)
    resid = k_ref - covar
    loss = lax.optimization_barrier(jnp.sum(ref_weight * resid * resid, axis=1))
    weighted = 2.0 * ref_weight * resid
    direct = weighted * k_ref
    back = -lax.dot_general(weighted, slab, (((1,), (1,)), ((), ())), precision=lax.Precision.HIGHEST, preferred_element_type=jnp.float32) * k_obs
    grad = jnp.dot(direct, ref_points, precision=lax.Precision.HIGHEST, preferred_element_type=jnp.float32)
    grad = grad + jnp.dot(back, observed, precision=lax.Precision.HIGHEST, preferred_element_type=jnp.float32)
    grad = grad - candidates * (lax.optimization_barrier(jnp.sum(direct, axis=1)) + lax.optimization_barrier(jnp.sum(back, axis=1)))[:, None]
    ascent = 32.0 / jnp.sqrt(jnp.float32(REFS)) * squared * grad
    return (ascent, loss / REFS)
```

```python
import functools

import jax
import jax.numpy as jnp
from jax import lax
from jax.experimental import pallas as pl
from jax.experimental.pallas import tpu as pltpu
from jax.sharding import PartitionSpec as P

F32, BF16 = jnp.float32, jnp.bfloat16
MESH = pl.DeviceIdType.MESH
CHUNK = 256
BLOCK = 256
ROWS = 1024
NT = (((1,), (1,)), ((), ()))
VMEM_BYTES = 60 * 1024 * 1024


def split(x):
    hi = x.astype(BF16)
    return hi, (x - hi.astype(F32)).astype(BF16)


def half_rows(own):
    return -(-own // 16) * 8


def mm(a, b):
    return jnp.dot(a, b, preferred_element_type=F32)


def mm_nt(a, b):
    return lax.dot_general(a, b, NT, preferred_element_type=F32)


def two_halves(x):
    hi = x.astype(BF16).astype(F32)
    return jnp.concatenate([hi, x - hi], axis=0).astype(BF16)


def kernel(n_dp, n_ref,
           cand_hbm, obs_hbm, refp_hbm, slab_ref, rw_hbm, inv_hbm,
           packed_ref,
           stage, s2, k2, kf, kt, kref, bmat, vnorm, o2, amat, unorm, cand_all,
           pbuf, a_recv, b_buf, b_recv, w_buf, w_recv, acc,
           gout, r_recv, d_send_buf, d_recv_buf, gt, dgrad, dloss,
           cand_ref, obs_ref, refp_ref, rw_ref, inv_ref, in_sem,
           slab_sem, g_ss, g_rs, a_ss, a_rs, b_ss, b_rs, c_ss, c_rs, r_ss, r_rs, d_ss, d_rs):
    dp, rf = lax.axis_index("dp"), lax.axis_index("ref")
    core, xi = lax.rem(dp, 2), dp // 2
    other = 1 - core
    partner = xi * 2 + other
    nx = n_dp // 2
    own, feat = cand_ref.shape
    q = own * n_ref
    half = q // 2
    obs_n, ref_n = slab_ref.shape
    nj = ref_n // CHUNK
    left = half_rows(own)

    def peer_ref(k):
        return (dp, lax.rem(rf + k, n_ref))

    def peer_dp(k):
        return (lax.rem(dp + k, n_dp), rf)

    def slab_copy(j):
        return pltpu.make_async_copy(
            slab_ref.at[:, pl.ds(pl.multiple_of(j * CHUNK, CHUNK), CHUNK)], stage.at[j], slab_sem.at[j])

    barrier = pltpu.get_barrier_semaphore()
    for k in range(1, n_ref):
        pl.semaphore_signal(barrier, inc=1, device_id=peer_ref(k), device_id_type=MESH)
    for k in range(1, n_dp):
        pl.semaphore_signal(barrier, inc=1, device_id=peer_dp(k), device_id_type=MESH)

    pairs = ((inv_hbm, inv_ref), (obs_hbm, obs_ref), (cand_hbm, cand_ref), (refp_hbm, refp_ref), (rw_hbm, rw_ref))
    inputs = [pltpu.make_async_copy(src, dst, in_sem.at[i]) for i, (src, dst) in enumerate(pairs)]
    for copy in inputs:
        copy.start()
    for j in range(nj):
        slab_copy(j).start()
    inputs[0].wait()
    inputs[1].wait()
    inv = inv_ref[...]
    inv_col = jnp.broadcast_to(inv, (8, feat)).T[:, 0:1]

    def prep(src, base, n):
        @pl.loop(0, n // BLOCK)
        def _(i):
            cols = pl.ds(pl.multiple_of(i * BLOCK, BLOCK), BLOCK)
            to = pl.ds(pl.multiple_of(base + i * BLOCK, BLOCK), BLOCK)
            v = src[:, cols]
            o2[0:2 * feat, to] = two_halves(v)
            o2[2 * feat:2 * feat + 16, to] = jnp.ones((16, BLOCK), BF16)
            sc = v * inv_col
            b1 = two_halves(sc)
            bmat[0:2 * feat, to] = b1
            bmat[2 * feat:4 * feat, to] = b1
            vnorm[:, to] = jnp.sum(sc * sc, axis=0, keepdims=True)

    prep(obs_ref, 0, obs_n)

    def split_slab(j):
        @pl.loop(0, obs_n // BLOCK)
        def _(i):
            rows = pl.ds(pl.multiple_of(i * BLOCK, BLOCK), BLOCK)
            hi, lo = split(stage[j, rows, :])
            s2[j, rows, 0:CHUNK] = hi
            s2[j, rows, CHUNK:2 * CHUNK] = lo

    for copy in inputs[2:]:
        copy.wait()
    pl.semaphore_wait(barrier, n_ref - 1 + n_dp - 1)

    def gather(k):
        return pltpu.make_async_remote_copy(
            src_ref=cand_ref, dst_ref=cand_all.at[rf], send_sem=g_ss.at[k], recv_sem=g_rs.at[k],
            device_id=peer_ref(k), device_id_type=MESH)

    for k in range(1, n_ref):
        gather(k).start()
    cand_all[rf] = cand_ref[...]

    prep(refp_ref, obs_n, ref_n)

    @pl.loop(0, nj)
    def _(j):
        slab_copy(j).wait()
        split_slab(j)

    for k in range(1, n_ref):
        gather(k).wait()

    u = cand_all[...].reshape(q, feat) * inv
    unorm[...] = jnp.sum(u * u, axis=1, keepdims=True)
    hi, lo = split(jnp.concatenate([u, u], axis=1))
    amat[:, 0:2 * feat] = hi
    amat[:, 2 * feat:4 * feat] = lo

    def kvals(start):
        rows = pl.ds(pl.multiple_of(start, BLOCK), BLOCK)
        cross = mm(amat[...], bmat[:, rows])
        return jnp.exp(-0.5 * (unorm[...] + vnorm[:, rows] - 2.0 * cross))

    @pl.loop(0, obs_n // BLOCK)
    def _(i):
        cols = pl.ds(pl.multiple_of(i * BLOCK, BLOCK), BLOCK)
        kk = kvals(i * BLOCK)
        kf[:, cols] = kk
        khi, klo = split(kk)
        k2[:, 0:half, cols] = khi.reshape(2, half, BLOCK)
        k2[:, half:q, cols] = klo.reshape(2, half, BLOCK)

    def a_copy(j):
        return pltpu.make_async_remote_copy(
            src_ref=pbuf.at[j, other], dst_ref=a_recv.at[j], send_sem=a_ss.at[j], recv_sem=a_rs.at[j],
            device_id=(partner, rf), device_id_type=MESH)

    def b_copy(j, m):
        return pltpu.make_async_remote_copy(
            src_ref=b_buf.at[j], dst_ref=b_recv.at[j, m - 1], send_sem=b_ss.at[j, m], recv_sem=b_rs.at[j, m],
            device_id=(lax.rem(xi + m, nx) * 2 + core, rf), device_id_type=MESH)

    def c_copy(j):
        return pltpu.make_async_remote_copy(
            src_ref=w_buf.at[j], dst_ref=w_recv.at[j], send_sem=c_ss.at[j], recv_sem=c_rs.at[j],
            device_id=(partner, rf), device_id_type=MESH)

    def finish_a(j):
        a_copy(j).wait()
        b_buf[j] = pbuf[j, core] + a_recv[j]
        for m in range(1, nx):
            b_copy(j, m).start()

    def first(j, h):
        x = mm(k2[h], s2[j, :, 0:CHUNK])
        pbuf[j, h] = x[0:half] + x[half:q] + mm(k2[h, 0:half, :], s2[j, :, CHUNK:2 * CHUNK])

    @pl.loop(0, nj)
    def _(j):
        first(j, other)
        a_copy(j).start()
        first(j, core)
        finish_a(j)

    @pl.loop(0, ref_n // BLOCK)
    def _(i):
        cols = pl.ds(pl.multiple_of(i * BLOCK, BLOCK), BLOCK)
        kref[:, :, cols] = kvals(obs_n + i * BLOCK).reshape(2, half, BLOCK)

    @pl.loop(0, obs_n // BLOCK)
    def _(i):
        rows = pl.ds(pl.multiple_of(i * BLOCK, BLOCK), BLOCK)
        kt[rows, :] = kf[:, rows].T

    gt[...] = jnp.zeros_like(gt)
    gout[...] = jnp.zeros_like(gout)

    def second(j):
        c_copy(j).wait()
        w, wr = w_buf[j], w_recv[j]
        low = core == 0
        wt = jnp.concatenate([jnp.where(low, w, wr), jnp.where(low, wr, w)], axis=0).T
        whi, wlo = split(wt)
        whl = jnp.concatenate([whi, wlo], axis=1)

        @pl.loop(0, obs_n // ROWS)
        def _(i):
            rows = pl.ds(pl.multiple_of(i * ROWS, ROWS), ROWS)
            x = mm(s2[j, rows, 0:CHUNK], whl)
            prod = x[:, 0:q] + x[:, q:2 * q] + mm(s2[j, rows, CHUNK:2 * CHUNK], whi)
            if j > 0:
                prod = acc[rows, :] + prod
            if j < nj - 1:
                acc[rows, :] = prod
            else:
                back = -prod * kt[rows, :]
                bhi, blo = split(back)
                pts = o2[:, rows]
                gt[...] += mm(pts, bhi) + mm(pts, blo)

    for j in range(nj):
        cols = slice(j * CHUNK, (j + 1) * CHUNK)
        for m in range(1, nx):
            b_copy(j, m).wait()
        total = b_buf[j]
        for m in range(1, nx):
            total = total + b_recv[j, m - 1]
        kr = kref[core, :, cols]
        rw = rw_ref[0:1, cols]
        resid = kr - total
        w = 2.0 * rw * resid
        w_buf[j] = w
        c_copy(j).start()
        dhi, dlo = split(w * kr)
        pts = o2[:, obs_n + j * CHUNK:obs_n + (j + 1) * CHUNK]
        dg = mm_nt(dhi, pts) + mm_nt(dlo, pts)
        dl = rw * resid * resid
        if j == 0:
            dgrad[...], dloss[...] = dg, dl
        else:
            dgrad[...] += dg
            dloss[...] += dl
        if j > 0:
            second(j - 1)
    second(nj - 1)

    def combine(g, cands):
        return g[:, 0:feat] + g[:, feat:2 * feat] - cands * g[:, 2 * feat:2 * feat + 1]

    grad = combine(gt[...].T, cand_all[...].reshape(q, feat))
    hslots = n_ref // 2
    mask = (xi == 0).astype(F32)
    extra = combine(dgrad[...], cand_all[pl.ds(core * hslots, hslots)].reshape(half, feat)) * mask
    loss = jnp.sum(dloss[...].T, axis=0, keepdims=True) * mask
    rest = own - left
    for i in range(n_ref):
        at = i * own
        gout[i, 0:left, 0:feat] = grad[at:at + left]
        gout[i, 0:rest, feat:2 * feat] = grad[at + left:at + own]
    for i in range(hslots):
        at, slot = i * own, core * hslots + i
        gout[slot, 0:left, 0:feat] += extra[at:at + left]
        gout[slot, 0:rest, feat:2 * feat] += extra[at + left:at + own]
        gout[slot, left:left + 1, 0:own] = loss[:, at:at + own]

    def r_copy(k):
        return pltpu.make_async_remote_copy(
            src_ref=gout.at[lax.rem(rf + k, n_ref)], dst_ref=r_recv.at[k - 1],
            send_sem=r_ss.at[k], recv_sem=r_rs.at[k], device_id=peer_ref(k), device_id_type=MESH)

    def d_copy(k):
        return pltpu.make_async_remote_copy(
            src_ref=d_send_buf, dst_ref=d_recv_buf.at[k],
            send_sem=d_ss.at[k], recv_sem=d_rs.at[k], device_id=peer_dp(k), device_id_type=MESH)

    for k in range(1, n_ref):
        r_copy(k).start()
    total = gout[rf]
    for k in range(1, n_ref):
        r_copy(k).wait()
        total = total + r_recv[k - 1]
    d_send_buf[...] = total
    for k in range(1, n_dp):
        d_copy(k).start()
    d_recv_buf[0] = total
    for k in range(1, n_dp):
        d_copy(k).wait()
    result = d_recv_buf[dp]
    for i in range(1, n_dp):
        result = result + d_recv_buf[lax.rem(dp - i + n_dp, n_dp)]
    packed_ref[...] = result


def finish(refs_total, packed_ref, inv_ref, ascent_ref, value_ref):
    feat = inv_ref.shape[1]
    own = ascent_ref.shape[0]
    left = half_rows(own)
    inv = inv_ref[...]
    scale = 32.0 / jnp.sqrt(F32(refs_total)) * (inv * inv)
    ascent_ref[0:left, :] = scale * packed_ref[0:left, 0:feat]
    ascent_ref[left:own, :] = scale * packed_ref[0:own - left, feat:2 * feat]
    value_ref[...] = packed_ref[left:left + 1, 0:own] / refs_total


def body(candidates, observed, ref_points, slab, ref_weight, inv_scale):
    n_ref, n_dp = lax.axis_size("ref"), lax.axis_size("dp")
    own, feat = candidates.shape
    q = own * n_ref
    half = q // 2
    obs_n, ref_n = slab.shape
    nj, nx = ref_n // CHUNK, n_dp // 2
    rows = half_rows(own) + 8
    vm = pl.BlockSpec(memory_space=pltpu.VMEM)
    V = pltpu.VMEM
    dma = pltpu.SemaphoreType.DMA
    inv_row = inv_scale.reshape(1, feat)
    packed = pl.pallas_call(
        functools.partial(kernel, n_dp, n_ref),
        out_shape=jax.ShapeDtypeStruct((rows, 128), F32),
        in_specs=[pl.BlockSpec(memory_space=pl.ANY)] * 6,
        out_specs=vm,
        scratch_shapes=[
            V((nj, obs_n, CHUNK), F32), V((nj, obs_n, 2 * CHUNK), BF16),
            V((2, q, obs_n), BF16), V((q, obs_n), F32), V((obs_n, q), F32), V((2, half, ref_n), F32),
            V((4 * feat, obs_n + ref_n), BF16), V((1, obs_n + ref_n), F32), V((2 * feat + 16, obs_n + ref_n), BF16),
            V((q, 4 * feat), BF16), V((q, 1), F32), V((n_ref, own, feat), F32),
            V((nj, 2, half, CHUNK), F32), V((nj, half, CHUNK), F32), V((nj, half, CHUNK), F32),
            V((nj, max(nx - 1, 1), half, CHUNK), F32), V((nj, half, CHUNK), F32), V((nj, half, CHUNK), F32),
            V((obs_n, q), F32),
            V((n_ref, rows, 128), F32), V((n_ref - 1, rows, 128), F32), V((rows, 128), F32), V((n_dp, rows, 128), F32),
            V((2 * feat + 16, q), F32), V((half, 2 * feat + 16), F32), V((half, CHUNK), F32),
            V((own, feat), F32), V((feat, obs_n), F32), V((feat, ref_n), F32), V((1, ref_n), F32), V((1, feat), F32), dma((5,)),
            dma((nj,)), dma((n_ref,)), dma((n_ref,)), dma((nj,)), dma((nj,)),
            dma((nj, nx)), dma((nj, nx)), dma((nj,)), dma((nj,)),
            dma((n_ref,)), dma((n_ref,)), dma((n_dp,)), dma((n_dp,)),
        ],
        compiler_params=pltpu.CompilerParams(
            collective_id=0, has_side_effects=True, vmem_limit_bytes=VMEM_BYTES),
        name="variance_grad",
    )(candidates, observed.T, ref_points.T, slab, ref_weight.reshape(1, ref_n), inv_row)
    ascent, value = pl.pallas_call(
        functools.partial(finish, ref_n * n_ref),
        out_shape=(jax.ShapeDtypeStruct((own, feat), F32), jax.ShapeDtypeStruct((1, own), F32)),
        in_specs=[vm, vm],
        out_specs=(vm, vm),
        name="scale_out",
    )(packed, inv_row)
    return ascent, value.reshape(own)


def solution(mesh):
    in_specs = (P("ref", None), P("dp", None), P("ref", None), P("dp", "ref"), P("ref"), P())
    out_specs = (P("ref", None), P("ref"))
    return jax.shard_map(body, mesh=mesh, in_specs=in_specs, out_specs=out_specs, check_vma=False)
```

```python
import functools

import jax
import jax.numpy as jnp
from jax import lax
from jax.experimental import pallas as pl
from jax.experimental.pallas import tpu as pltpu
from jax.sharding import PartitionSpec as P

F32, BF16 = jnp.float32, jnp.bfloat16
MESH = pl.DeviceIdType.MESH
CHUNK = 256
BLOCK = 256
KBLOCK = 1024
ROWS = 1024
NT = (((1,), (1,)), ((), ()))
VMEM_BYTES = 60 * 1024 * 1024


def split(x):
    hi = x.astype(BF16)
    return hi, (x - hi.astype(F32)).astype(BF16)


def half_rows(own):
    return -(-own // 16) * 8


def mm(a, b):
    return jnp.dot(a, b, preferred_element_type=F32)


def mm_nt(a, b):
    return lax.dot_general(a, b, NT, preferred_element_type=F32)


def two_halves(x):
    hi = x.astype(BF16).astype(F32)
    return jnp.concatenate([hi, x - hi], axis=0).astype(BF16)


def kernel(n_dp, n_ref,
           cand_hbm, obs_hbm, refp_hbm, slab_ref, rw_hbm, inv_hbm,
           packed_ref,
           stage, s2, k2, kf, kt, kref, bmat, vnorm, o2, amat, unorm, cand_all,
           pbuf, a_recv, b_buf, b_recv, w_buf, w_recv, acc,
           gout, r_recv, d_send_buf, d_recv_buf, gt, dgrad, dloss,
           cand_ref, obs_ref, refp_ref, rw_ref, inv_ref, in_sem,
           slab_sem, g_ss, g_rs, a_ss, a_rs, b_ss, b_rs, c_ss, c_rs, r_ss, r_rs, d_ss, d_rs):
    dp, rf = lax.axis_index("dp"), lax.axis_index("ref")
    core, xi = lax.rem(dp, 2), dp // 2
    other = 1 - core
    partner = xi * 2 + other
    nx = n_dp // 2
    own, feat = cand_ref.shape
    q = own * n_ref
    half = q // 2
    obs_n, ref_n = slab_ref.shape
    nj = ref_n // CHUNK
    left = half_rows(own)

    def peer_ref(k):
        return (dp, lax.rem(rf + k, n_ref))

    def peer_dp(k):
        return (lax.rem(dp + k, n_dp), rf)

    def slab_copy(j):
        return pltpu.make_async_copy(
            slab_ref.at[:, pl.ds(pl.multiple_of(j * CHUNK, CHUNK), CHUNK)], stage.at[j], slab_sem.at[j])

    barrier = pltpu.get_barrier_semaphore()
    for k in range(1, n_ref):
        pl.semaphore_signal(barrier, inc=1, device_id=peer_ref(k), device_id_type=MESH)
    for k in range(1, n_dp):
        pl.semaphore_signal(barrier, inc=1, device_id=peer_dp(k), device_id_type=MESH)

    pairs = ((inv_hbm, inv_ref), (obs_hbm, obs_ref), (cand_hbm, cand_ref), (refp_hbm, refp_ref), (rw_hbm, rw_ref))
    inputs = [pltpu.make_async_copy(src, dst, in_sem.at[i]) for i, (src, dst) in enumerate(pairs)]
    for copy in inputs:
        copy.start()
    for j in range(nj):
        slab_copy(j).start()
    inputs[0].wait()
    inputs[1].wait()
    inv = inv_ref[...]
    inv_col = jnp.broadcast_to(inv, (8, feat)).T[:, 0:1]

    def prep(src, base, n):
        @pl.loop(0, n // BLOCK)
        def _(i):
            cols = pl.ds(pl.multiple_of(i * BLOCK, BLOCK), BLOCK)
            to = pl.ds(pl.multiple_of(base + i * BLOCK, BLOCK), BLOCK)
            v = src[:, cols]
            o2[0:2 * feat, to] = two_halves(v)
            o2[2 * feat:2 * feat + 16, to] = jnp.ones((16, BLOCK), BF16)
            sc = v * inv_col
            b1 = two_halves(sc)
            bmat[0:2 * feat, to] = b1
            bmat[2 * feat:4 * feat, to] = b1
            vnorm[:, to] = jnp.sum(sc * sc, axis=0, keepdims=True)

    prep(obs_ref, 0, obs_n)

    def split_slab(j):
        @pl.loop(0, obs_n // BLOCK)
        def _(i):
            rows = pl.ds(pl.multiple_of(i * BLOCK, BLOCK), BLOCK)
            hi, lo = split(stage[j, rows, :])
            s2[j, rows, 0:CHUNK] = hi
            s2[j, rows, CHUNK:2 * CHUNK] = lo

    for copy in inputs[2:]:
        copy.wait()
    pl.semaphore_wait(barrier, n_ref - 1 + n_dp - 1)

    def gather(k):
        return pltpu.make_async_remote_copy(
            src_ref=cand_ref, dst_ref=cand_all.at[rf], send_sem=g_ss.at[k], recv_sem=g_rs.at[k],
            device_id=peer_ref(k), device_id_type=MESH)

    for k in range(1, n_ref):
        gather(k).start()
    cand_all[rf] = cand_ref[...]

    prep(refp_ref, obs_n, ref_n)

    @pl.loop(0, nj)
    def _(j):
        slab_copy(j).wait()
        split_slab(j)

    for k in range(1, n_ref):
        gather(k).wait()

    u = cand_all[...].reshape(q, feat) * inv
    unorm[...] = jnp.sum(u * u, axis=1, keepdims=True)
    hi, lo = split(jnp.concatenate([u, u], axis=1))
    amat[:, 0:2 * feat] = hi
    amat[:, 2 * feat:4 * feat] = lo

    def kvals(start):
        rows = pl.ds(pl.multiple_of(start, KBLOCK), KBLOCK)
        cross = mm(amat[...], bmat[:, rows])
        return jnp.exp(-0.5 * (unorm[...] + vnorm[:, rows] - 2.0 * cross))

    @pl.loop(0, obs_n // KBLOCK)
    def _(i):
        cols = pl.ds(pl.multiple_of(i * KBLOCK, KBLOCK), KBLOCK)
        kk = kvals(i * KBLOCK)
        kf[:, cols] = kk
        khi, klo = split(kk)
        k2[:, 0:half, cols] = khi.reshape(2, half, KBLOCK)
        k2[:, half:q, cols] = klo.reshape(2, half, KBLOCK)

    def a_copy(j):
        return pltpu.make_async_remote_copy(
            src_ref=pbuf.at[j, other], dst_ref=a_recv.at[j], send_sem=a_ss.at[j], recv_sem=a_rs.at[j],
            device_id=(partner, rf), device_id_type=MESH)

    def b_copy(j, m):
        return pltpu.make_async_remote_copy(
            src_ref=b_buf.at[j], dst_ref=b_recv.at[j, m - 1], send_sem=b_ss.at[j, m], recv_sem=b_rs.at[j, m],
            device_id=(lax.rem(xi + m, nx) * 2 + core, rf), device_id_type=MESH)

    def c_copy(j):
        return pltpu.make_async_remote_copy(
            src_ref=w_buf.at[j], dst_ref=w_recv.at[j], send_sem=c_ss.at[j], recv_sem=c_rs.at[j],
            device_id=(partner, rf), device_id_type=MESH)

    def finish_a(j):
        a_copy(j).wait()
        b_buf[j] = pbuf[j, core] + a_recv[j]
        for m in range(1, nx):
            b_copy(j, m).start()

    def first(j, h):
        x = mm(k2[h], s2[j, :, 0:CHUNK])
        pbuf[j, h] = x[0:half] + x[half:q] + mm(k2[h, 0:half, :], s2[j, :, CHUNK:2 * CHUNK])

    @pl.loop(0, nj)
    def _(j):
        first(j, other)
        a_copy(j).start()
        first(j, core)
        finish_a(j)

    @pl.loop(0, ref_n // KBLOCK)
    def _(i):
        cols = pl.ds(pl.multiple_of(i * KBLOCK, KBLOCK), KBLOCK)
        kref[:, :, cols] = kvals(obs_n + i * KBLOCK).reshape(2, half, KBLOCK)

    @pl.loop(0, obs_n // BLOCK)
    def _(i):
        rows = pl.ds(pl.multiple_of(i * BLOCK, BLOCK), BLOCK)
        kt[rows, :] = kf[:, rows].T

    gt[...] = jnp.zeros_like(gt)
    gout[...] = jnp.zeros_like(gout)

    def second(j):
        c_copy(j).wait()
        w, wr = w_buf[j], w_recv[j]
        low = core == 0
        wt = jnp.concatenate([jnp.where(low, w, wr), jnp.where(low, wr, w)], axis=0).T
        whi, wlo = split(wt)
        whl = jnp.concatenate([whi, wlo], axis=1)

        @pl.loop(0, obs_n // ROWS)
        def _(i):
            rows = pl.ds(pl.multiple_of(i * ROWS, ROWS), ROWS)
            x = mm(s2[j, rows, 0:CHUNK], whl)
            prod = x[:, 0:q] + x[:, q:2 * q] + mm(s2[j, rows, CHUNK:2 * CHUNK], whi)
            if j > 0:
                prod = acc[rows, :] + prod
            if j < nj - 1:
                acc[rows, :] = prod
            else:
                back = -prod * kt[rows, :]
                bhi, blo = split(back)
                pts = o2[:, rows]
                gt[...] += mm(pts, bhi) + mm(pts, blo)

    hslots = n_ref // 2
    rest = own - left

    def combine(g, cands):
        return g[:, 0:feat] + g[:, feat:2 * feat] - cands * g[:, 2 * feat:2 * feat + 1]

    def stage_direct():
        mask = (xi == 0).astype(F32)
        extra = combine(dgrad[...], cand_all[pl.ds(core * hslots, hslots)].reshape(half, feat)) * mask
        loss = jnp.sum(dloss[...].T, axis=0, keepdims=True) * mask
        for i in range(hslots):
            at, slot = i * own, core * hslots + i
            gout[slot, 0:left, 0:feat] = extra[at:at + left]
            gout[slot, 0:rest, feat:2 * feat] = extra[at + left:at + own]
            gout[slot, left:left + 1, 0:own] = loss[:, at:at + own]

    for j in range(nj):
        cols = slice(j * CHUNK, (j + 1) * CHUNK)
        for m in range(1, nx):
            b_copy(j, m).wait()
        total = b_buf[j]
        for m in range(1, nx):
            total = total + b_recv[j, m - 1]
        kr = kref[core, :, cols]
        rw = rw_ref[0:1, cols]
        resid = kr - total
        w = 2.0 * rw * resid
        w_buf[j] = w
        c_copy(j).start()
        dhi, dlo = split(w * kr)
        pts = o2[:, obs_n + j * CHUNK:obs_n + (j + 1) * CHUNK]
        dg = mm_nt(dhi, pts) + mm_nt(dlo, pts)
        dl = rw * resid * resid
        if j == 0:
            dgrad[...], dloss[...] = dg, dl
        else:
            dgrad[...] += dg
            dloss[...] += dl
        if j > 0:
            second(j - 1)
    stage_direct()
    second(nj - 1)

    grad = combine(gt[...].T, cand_all[...].reshape(q, feat))
    for i in range(n_ref):
        at = i * own
        gout[i, 0:left, 0:feat] += grad[at:at + left]
        gout[i, 0:rest, feat:2 * feat] += grad[at + left:at + own]

    def r_copy(k):
        return pltpu.make_async_remote_copy(
            src_ref=gout.at[lax.rem(rf + k, n_ref)], dst_ref=r_recv.at[k - 1],
            send_sem=r_ss.at[k], recv_sem=r_rs.at[k], device_id=peer_ref(k), device_id_type=MESH)

    def d_copy(k):
        return pltpu.make_async_remote_copy(
            src_ref=d_send_buf, dst_ref=d_recv_buf.at[k],
            send_sem=d_ss.at[k], recv_sem=d_rs.at[k], device_id=peer_dp(k), device_id_type=MESH)

    for k in range(1, n_ref):
        r_copy(k).start()
    total = gout[rf]
    for k in range(1, n_ref):
        r_copy(k).wait()
        total = total + r_recv[k - 1]
    d_send_buf[...] = total
    for k in range(1, n_dp):
        d_copy(k).start()
    d_recv_buf[0] = total
    for k in range(1, n_dp):
        d_copy(k).wait()
    result = d_recv_buf[dp]
    for i in range(1, n_dp):
        result = result + d_recv_buf[lax.rem(dp - i + n_dp, n_dp)]
    packed_ref[...] = result


def finish(refs_total, packed_ref, inv_ref, ascent_ref, value_ref):
    feat = inv_ref.shape[1]
    own = ascent_ref.shape[0]
    left = half_rows(own)
    inv = inv_ref[...]
    scale = 32.0 / jnp.sqrt(F32(refs_total)) * (inv * inv)
    ascent_ref[0:left, :] = scale * packed_ref[0:left, 0:feat]
    ascent_ref[left:own, :] = scale * packed_ref[0:own - left, feat:2 * feat]
    value_ref[...] = packed_ref[left:left + 1, 0:own] / refs_total


def body(candidates, observed, ref_points, slab, ref_weight, inv_scale):
    n_ref, n_dp = lax.axis_size("ref"), lax.axis_size("dp")
    own, feat = candidates.shape
    q = own * n_ref
    half = q // 2
    obs_n, ref_n = slab.shape
    nj, nx = ref_n // CHUNK, n_dp // 2
    rows = half_rows(own) + 8
    vm = pl.BlockSpec(memory_space=pltpu.VMEM)
    V = pltpu.VMEM
    dma = pltpu.SemaphoreType.DMA
    inv_row = inv_scale.reshape(1, feat)
    packed = pl.pallas_call(
        functools.partial(kernel, n_dp, n_ref),
        out_shape=jax.ShapeDtypeStruct((rows, 128), F32),
        in_specs=[pl.BlockSpec(memory_space=pl.ANY)] * 6,
        out_specs=vm,
        scratch_shapes=[
            V((nj, obs_n, CHUNK), F32), V((nj, obs_n, 2 * CHUNK), BF16),
            V((2, q, obs_n), BF16), V((q, obs_n), F32), V((obs_n, q), F32), V((2, half, ref_n), F32),
            V((4 * feat, obs_n + ref_n), BF16), V((1, obs_n + ref_n), F32), V((2 * feat + 16, obs_n + ref_n), BF16),
            V((q, 4 * feat), BF16), V((q, 1), F32), V((n_ref, own, feat), F32),
            V((nj, 2, half, CHUNK), F32), V((nj, half, CHUNK), F32), V((nj, half, CHUNK), F32),
            V((nj, max(nx - 1, 1), half, CHUNK), F32), V((nj, half, CHUNK), F32), V((nj, half, CHUNK), F32),
            V((obs_n, q), F32),
            V((n_ref, rows, 128), F32), V((n_ref - 1, rows, 128), F32), V((rows, 128), F32), V((n_dp, rows, 128), F32),
            V((2 * feat + 16, q), F32), V((half, 2 * feat + 16), F32), V((half, CHUNK), F32),
            V((own, feat), F32), V((feat, obs_n), F32), V((feat, ref_n), F32), V((1, ref_n), F32), V((1, feat), F32), dma((5,)),
            dma((nj,)), dma((n_ref,)), dma((n_ref,)), dma((nj,)), dma((nj,)),
            dma((nj, nx)), dma((nj, nx)), dma((nj,)), dma((nj,)),
            dma((n_ref,)), dma((n_ref,)), dma((n_dp,)), dma((n_dp,)),
        ],
        compiler_params=pltpu.CompilerParams(
            collective_id=0, has_side_effects=True, vmem_limit_bytes=VMEM_BYTES),
        name="variance_grad",
    )(candidates, observed.T, ref_points.T, slab, ref_weight.reshape(1, ref_n), inv_row)
    ascent, value = pl.pallas_call(
        functools.partial(finish, ref_n * n_ref),
        out_shape=(jax.ShapeDtypeStruct((own, feat), F32), jax.ShapeDtypeStruct((1, own), F32)),
        in_specs=[vm, vm],
        out_specs=(vm, vm),
        name="scale_out",
    )(packed, inv_row)
    return ascent, value.reshape(own)


def solution(mesh):
    in_specs = (P("ref", None), P("dp", None), P("ref", None), P("dp", "ref"), P("ref"), P())
    out_specs = (P("ref", None), P("ref"))
    return jax.shard_map(body, mesh=mesh, in_specs=in_specs, out_specs=out_specs, check_vma=False)
```

```python
import functools

import jax
import jax.numpy as jnp
from jax import lax
from jax.experimental import pallas as pl
from jax.experimental.pallas import tpu as pltpu
from jax.sharding import PartitionSpec as P

F32, BF16 = jnp.float32, jnp.bfloat16
MESH = pl.DeviceIdType.MESH
CHUNK = 256
BLOCK = 256
KBLOCK = 1024
HEAD_ROWS = 1024
NT = (((1,), (1,)), ((), ()))
VMEM_BYTES = 60 * 1024 * 1024


def split(x):
    hi = x.astype(BF16)
    return hi, (x - hi.astype(F32)).astype(BF16)


def half_rows(own):
    return -(-own // 16) * 8


def mm(a, b):
    return jnp.dot(a, b, preferred_element_type=F32)


def mm_nt(a, b):
    return lax.dot_general(a, b, NT, preferred_element_type=F32)


def two_halves(x):
    hi = x.astype(BF16).astype(F32)
    return jnp.concatenate([hi, x - hi], axis=0).astype(BF16)


def kernel(n_dp, n_ref,
           cand_hbm, obs_hbm, refp_hbm, slab_ref, rw_hbm, inv_hbm,
           packed_ref,
           stage, s_hi, s_lo, w_t, k2, kf, kt, kref, bmat, vnorm, o2, amat, unorm, cand_all,
           pbuf, a_recv, b_buf, b_recv, w_buf, w_recv, acc,
           gout, r_recv, d_send_buf, d_recv_buf, gt, dgrad, dloss,
           cand_ref, obs_ref, refp_ref, rw_ref, inv_ref, in_sem,
           slab_sem, g_ss, g_rs, a_ss, a_rs, b_ss, b_rs, c_ss, c_rs, r_ss, r_rs, d_ss, d_rs):
    dp, rf = lax.axis_index("dp"), lax.axis_index("ref")
    core, xi = lax.rem(dp, 2), dp // 2
    other = 1 - core
    partner = xi * 2 + other
    nx = n_dp // 2
    own, feat = cand_ref.shape
    q = own * n_ref
    half = q // 2
    obs_n, ref_n = slab_ref.shape
    nj = ref_n // CHUNK
    left = half_rows(own)

    def peer_ref(k):
        return (dp, lax.rem(rf + k, n_ref))

    def peer_dp(k):
        return (lax.rem(dp + k, n_dp), rf)

    def slab_copy(j):
        return pltpu.make_async_copy(
            slab_ref.at[:, pl.ds(pl.multiple_of(j * CHUNK, CHUNK), CHUNK)], stage.at[j], slab_sem.at[j])

    barrier = pltpu.get_barrier_semaphore()
    for k in range(1, n_ref):
        pl.semaphore_signal(barrier, inc=1, device_id=peer_ref(k), device_id_type=MESH)
    for k in range(1, n_dp):
        pl.semaphore_signal(barrier, inc=1, device_id=peer_dp(k), device_id_type=MESH)

    pairs = ((inv_hbm, inv_ref), (obs_hbm, obs_ref), (cand_hbm, cand_ref), (refp_hbm, refp_ref), (rw_hbm, rw_ref))
    inputs = [pltpu.make_async_copy(src, dst, in_sem.at[i]) for i, (src, dst) in enumerate(pairs)]
    for copy in inputs:
        copy.start()
    for j in range(nj):
        slab_copy(j).start()
    inputs[0].wait()
    inputs[1].wait()
    inv = inv_ref[...]
    inv_col = jnp.broadcast_to(inv, (8, feat)).T[:, 0:1]

    def prep(src, base, n):
        @pl.loop(0, n // BLOCK)
        def _(i):
            cols = pl.ds(pl.multiple_of(i * BLOCK, BLOCK), BLOCK)
            to = pl.ds(pl.multiple_of(base + i * BLOCK, BLOCK), BLOCK)
            v = src[:, cols]
            o2[0:2 * feat, to] = two_halves(v)
            o2[2 * feat:2 * feat + 16, to] = jnp.ones((16, BLOCK), BF16)
            sc = v * inv_col
            b1 = two_halves(sc)
            bmat[0:2 * feat, to] = b1
            bmat[2 * feat:4 * feat, to] = b1
            vnorm[:, to] = jnp.sum(sc * sc, axis=0, keepdims=True)

    prep(obs_ref, 0, obs_n)

    def split_slab(j):
        cols = pl.ds(pl.multiple_of(j * CHUNK, CHUNK), CHUNK)

        @pl.loop(0, obs_n // BLOCK)
        def _(i):
            rows = pl.ds(pl.multiple_of(i * BLOCK, BLOCK), BLOCK)
            hi, lo = split(stage[j, rows, :])
            s_hi[rows, cols] = hi
            s_lo[rows, cols] = lo

    for copy in inputs[2:]:
        copy.wait()
    pl.semaphore_wait(barrier, n_ref - 1 + n_dp - 1)

    def gather(k):
        return pltpu.make_async_remote_copy(
            src_ref=cand_ref, dst_ref=cand_all.at[rf], send_sem=g_ss.at[k], recv_sem=g_rs.at[k],
            device_id=peer_ref(k), device_id_type=MESH)

    for k in range(1, n_ref):
        gather(k).start()
    cand_all[rf] = cand_ref[...]

    prep(refp_ref, obs_n, ref_n)

    @pl.loop(0, nj)
    def _(j):
        slab_copy(j).wait()
        split_slab(j)

    for k in range(1, n_ref):
        gather(k).wait()

    u = cand_all[...].reshape(q, feat) * inv
    unorm[...] = jnp.sum(u * u, axis=1, keepdims=True)
    hi, lo = split(jnp.concatenate([u, u], axis=1))
    amat[:, 0:2 * feat] = hi
    amat[:, 2 * feat:4 * feat] = lo

    def kvals(start):
        rows = pl.ds(pl.multiple_of(start, KBLOCK), KBLOCK)
        cross = mm(amat[...], bmat[:, rows])
        return jnp.exp(-0.5 * (unorm[...] + vnorm[:, rows] - 2.0 * cross))

    @pl.loop(0, obs_n // KBLOCK)
    def _(i):
        cols = pl.ds(pl.multiple_of(i * KBLOCK, KBLOCK), KBLOCK)
        kk = kvals(i * KBLOCK)
        kf[:, cols] = kk
        khi, klo = split(kk)
        k2[0:q, cols] = khi
        k2[q:2 * q, cols] = klo

    def a_copy(j):
        return pltpu.make_async_remote_copy(
            src_ref=pbuf.at[j, other], dst_ref=a_recv.at[j], send_sem=a_ss.at[j], recv_sem=a_rs.at[j],
            device_id=(partner, rf), device_id_type=MESH)

    def b_copy(j, m):
        return pltpu.make_async_remote_copy(
            src_ref=b_buf.at[j], dst_ref=b_recv.at[j, m - 1], send_sem=b_ss.at[j, m], recv_sem=b_rs.at[j, m],
            device_id=(lax.rem(xi + m, nx) * 2 + core, rf), device_id_type=MESH)

    def c_copy(j):
        return pltpu.make_async_remote_copy(
            src_ref=w_buf.at[j], dst_ref=w_recv.at[j], send_sem=c_ss.at[j], recv_sem=c_rs.at[j],
            device_id=(partner, rf), device_id_type=MESH)

    def finish_a(j):
        a_copy(j).wait()
        b_buf[j] = pbuf[j, core] + a_recv[j]
        for m in range(1, nx):
            b_copy(j, m).start()

    def first(j):
        cols = pl.ds(pl.multiple_of(j * CHUNK, CHUNK), CHUNK)
        x = mm(k2[...], s_hi[:, cols])
        x = x[0:q] + x[q:2 * q] + mm(k2[0:q, :], s_lo[:, cols])
        pbuf[j] = x.reshape(2, half, CHUNK)

    @pl.loop(0, nj)
    def _(j):
        first(j)
        a_copy(j).start()

        @pl.when(j > 0)
        def _():
            finish_a(j - 1)

    finish_a(nj - 1)

    @pl.loop(0, ref_n // KBLOCK)
    def _(i):
        cols = pl.ds(pl.multiple_of(i * KBLOCK, KBLOCK), KBLOCK)
        kref[:, :, cols] = kvals(obs_n + i * KBLOCK).reshape(2, half, KBLOCK)

    @pl.loop(0, obs_n // BLOCK)
    def _(i):
        rows = pl.ds(pl.multiple_of(i * BLOCK, BLOCK), BLOCK)
        kt[rows, :] = kf[:, rows].T

    gout[...] = jnp.zeros_like(gout)

    def place(j):
        c_copy(j).wait()
        w, wr = w_buf[j], w_recv[j]
        low = core == 0
        wt = jnp.concatenate([jnp.where(low, w, wr), jnp.where(low, wr, w)], axis=0).T
        whi, wlo = split(wt)
        w_t[j * CHUNK:(j + 1) * CHUNK, 0:q] = whi
        w_t[j * CHUNK:(j + 1) * CHUNK, q:2 * q] = wlo

    head = max(nj - 2, 0) * CHUNK

    def second(rows, k0, k1):
        x = mm(s_hi[rows, k0:k1], w_t[k0:k1, :])
        return x[:, 0:q] + x[:, q:2 * q] + mm(s_lo[rows, k0:k1], w_t[k0:k1, 0:q])

    def second_head(j):
        @pl.loop(0, obs_n // HEAD_ROWS)
        def _(i):
            rows = pl.ds(pl.multiple_of(i * HEAD_ROWS, HEAD_ROWS), HEAD_ROWS)
            prod = second(rows, j * CHUNK, (j + 1) * CHUNK)
            if j > 0:
                prod = acc[rows, :] + prod
            acc[rows, :] = prod

    def second_last():
        prod = second(slice(0, obs_n), head, ref_n)
        if head > 0:
            prod = acc[...] + prod
        bhi, blo = split(-prod * kt[...])
        pts = o2[:, 0:obs_n]
        gt[...] = mm(pts, bhi) + mm(pts, blo)

    hslots = n_ref // 2
    rest = own - left

    def combine(g, cands):
        return g[:, 0:feat] + g[:, feat:2 * feat] - cands * g[:, 2 * feat:2 * feat + 1]

    def stage_direct():
        mask = (xi == 0).astype(F32)
        extra = combine(dgrad[...], cand_all[pl.ds(core * hslots, hslots)].reshape(half, feat)) * mask
        loss = jnp.sum(dloss[...].T, axis=0, keepdims=True) * mask
        for i in range(hslots):
            at, slot = i * own, core * hslots + i
            gout[slot, 0:left, 0:feat] = extra[at:at + left]
            gout[slot, 0:rest, feat:2 * feat] = extra[at + left:at + own]
            gout[slot, left:left + 1, 0:own] = loss[:, at:at + own]

    for j in range(nj):
        cols = slice(j * CHUNK, (j + 1) * CHUNK)
        for m in range(1, nx):
            b_copy(j, m).wait()
        total = b_buf[j]
        for m in range(1, nx):
            total = total + b_recv[j, m - 1]
        kr = kref[core, :, cols]
        rw = rw_ref[0:1, cols]
        resid = kr - total
        w = 2.0 * rw * resid
        w_buf[j] = w
        c_copy(j).start()
        dhi, dlo = split(w * kr)
        pts = o2[:, obs_n + j * CHUNK:obs_n + (j + 1) * CHUNK]
        dg = mm_nt(dhi, pts) + mm_nt(dlo, pts)
        dl = rw * resid * resid
        if j == 0:
            dgrad[...], dloss[...] = dg, dl
        else:
            dgrad[...] += dg
            dloss[...] += dl
        if j > 0:
            place(j - 1)
            if j < nj - 1:
                second_head(j - 1)
    stage_direct()
    place(nj - 1)
    second_last()

    grad = combine(gt[...].T, cand_all[...].reshape(q, feat))
    for i in range(n_ref):
        at = i * own
        gout[i, 0:left, 0:feat] += grad[at:at + left]
        gout[i, 0:rest, feat:2 * feat] += grad[at + left:at + own]

    def r_copy(k):
        return pltpu.make_async_remote_copy(
            src_ref=gout.at[lax.rem(rf + k, n_ref)], dst_ref=r_recv.at[k - 1],
            send_sem=r_ss.at[k], recv_sem=r_rs.at[k], device_id=peer_ref(k), device_id_type=MESH)

    def d_copy(k):
        return pltpu.make_async_remote_copy(
            src_ref=d_send_buf, dst_ref=d_recv_buf.at[k],
            send_sem=d_ss.at[k], recv_sem=d_rs.at[k], device_id=peer_dp(k), device_id_type=MESH)

    for k in range(1, n_ref):
        r_copy(k).start()
    total = gout[rf]
    for k in range(1, n_ref):
        r_copy(k).wait()
        total = total + r_recv[k - 1]
    d_send_buf[...] = total
    for k in range(1, n_dp):
        d_copy(k).start()
    d_recv_buf[0] = total
    for k in range(1, n_dp):
        d_copy(k).wait()
    result = d_recv_buf[dp]
    for i in range(1, n_dp):
        result = result + d_recv_buf[lax.rem(dp - i + n_dp, n_dp)]
    packed_ref[...] = result


def finish(refs_total, packed_ref, inv_ref, ascent_ref, value_ref):
    feat = inv_ref.shape[1]
    own = ascent_ref.shape[0]
    left = half_rows(own)
    inv = inv_ref[...]
    scale = 32.0 / jnp.sqrt(F32(refs_total)) * (inv * inv)
    ascent_ref[0:left, :] = scale * packed_ref[0:left, 0:feat]
    ascent_ref[left:own, :] = scale * packed_ref[0:own - left, feat:2 * feat]
    value_ref[...] = packed_ref[left:left + 1, 0:own] / refs_total


def body(candidates, observed, ref_points, slab, ref_weight, inv_scale):
    n_ref, n_dp = lax.axis_size("ref"), lax.axis_size("dp")
    own, feat = candidates.shape
    q = own * n_ref
    half = q // 2
    obs_n, ref_n = slab.shape
    nj, nx = ref_n // CHUNK, n_dp // 2
    rows = half_rows(own) + 8
    vm = pl.BlockSpec(memory_space=pltpu.VMEM)
    V = pltpu.VMEM
    dma = pltpu.SemaphoreType.DMA
    inv_row = inv_scale.reshape(1, feat)
    packed = pl.pallas_call(
        functools.partial(kernel, n_dp, n_ref),
        out_shape=jax.ShapeDtypeStruct((rows, 128), F32),
        in_specs=[pl.BlockSpec(memory_space=pl.ANY)] * 6,
        out_specs=vm,
        scratch_shapes=[
            V((nj, obs_n, CHUNK), F32), V((obs_n, ref_n), BF16), V((obs_n, ref_n), BF16), V((ref_n, 2 * q), BF16),
            V((2 * q, obs_n), BF16), V((q, obs_n), F32), V((obs_n, q), F32), V((2, half, ref_n), F32),
            V((4 * feat, obs_n + ref_n), BF16), V((1, obs_n + ref_n), F32), V((2 * feat + 16, obs_n + ref_n), BF16),
            V((q, 4 * feat), BF16), V((q, 1), F32), V((n_ref, own, feat), F32),
            V((nj, 2, half, CHUNK), F32), V((nj, half, CHUNK), F32), V((nj, half, CHUNK), F32),
            V((nj, max(nx - 1, 1), half, CHUNK), F32), V((nj, half, CHUNK), F32), V((nj, half, CHUNK), F32),
            V((obs_n, q), F32),
            V((n_ref, rows, 128), F32), V((n_ref - 1, rows, 128), F32), V((rows, 128), F32), V((n_dp, rows, 128), F32),
            V((2 * feat + 16, q), F32), V((half, 2 * feat + 16), F32), V((half, CHUNK), F32),
            V((own, feat), F32), V((feat, obs_n), F32), V((feat, ref_n), F32), V((1, ref_n), F32), V((1, feat), F32), dma((5,)),
            dma((nj,)), dma((n_ref,)), dma((n_ref,)), dma((nj,)), dma((nj,)),
            dma((nj, nx)), dma((nj, nx)), dma((nj,)), dma((nj,)),
            dma((n_ref,)), dma((n_ref,)), dma((n_dp,)), dma((n_dp,)),
        ],
        compiler_params=pltpu.CompilerParams(
            collective_id=0, has_side_effects=True, vmem_limit_bytes=VMEM_BYTES),
        name="variance_grad",
    )(candidates, observed.T, ref_points.T, slab, ref_weight.reshape(1, ref_n), inv_row)
    ascent, value = pl.pallas_call(
        functools.partial(finish, ref_n * n_ref),
        out_shape=(jax.ShapeDtypeStruct((own, feat), F32), jax.ShapeDtypeStruct((1, own), F32)),
        in_specs=[vm, vm],
        out_specs=(vm, vm),
        name="scale_out",
    )(packed, inv_row)
    return ascent, value.reshape(own)


def solution(mesh):
    in_specs = (P("ref", None), P("dp", None), P("ref", None), P("dp", "ref"), P("ref"), P())
    out_specs = (P("ref", None), P("ref"))
    return jax.shard_map(body, mesh=mesh, in_specs=in_specs, out_specs=out_specs, check_vma=False)
```
